256 devices in a mesh: head: 16 (over y_hi, z), ctx: 16 (over x, y_lo, core).
Axes of the slice: x: 4, y: 4 (y_hi: 2, y_lo: 2; y = y_hi * 2 + y_lo), z: 8, core: 2. Of those that a mesh axis runs over, the one named last changes fastest.
Arguments:
- queries: bfloat16 [8192, 2048], P(('ctx', 'head')), may hold values from -9 to 9
- keys: bfloat16 [8192, 8192], P('ctx', 'head'), may hold values from -9 to 9
- values: bfloat16 [8192, 8192], P('ctx', 'head'), may hold values from -6 to 6
- routes: int32 [8192, 16], P(('ctx', 'head')), may hold values from 0 to 63, all different within a row; in each aligned block of 32 rows (0 to 31, 32 to 63, ...) at most 16 rows name the same one
- gates: float32 [8192, 16], P(('ctx', 'head')), may hold values from 0.25 to 1
- block_mask: int32 [64, 64], replicated, may hold values 0 or 1
- w_out: bfloat16 [8192, 8192], P('head'), may hold values from -0.125 to 0.125
Outputs:
- mixed: bfloat16 [8192, 8192], P(('ctx', 'head'))
The draws below stay inside these ranges and needn't reach their ends.
Inputs may be any that keep to these rules, and one draw needn't show every extreme that they name: `routes`: in each aligned block of 32 rows (the rows of one device) no head is named more than 16 times; each row names 16 different heads.
All inputs are finite; a program needn't handle non-finite values.
Results may differ from the reference program's by a relative error of at most 0.015.
Values may be sent and summed in bfloat16 or wider, within the bound.
No kernel may reach another device: no remote copies, remote signals or barrier semaphores. Data moves between devices by JAX's collectives and lax.ppermute only.
A program may use at most 128 MiB of HBM per device.

```python
import math
import jax
import jax.numpy as jnp
import numpy as np
from jax import lax

D = 8192
H = 64
HD = 128
TOPH = 16
BLK = 128
TOK_DEV = 32
SEQ = 8192
CAP = 16
NB = 64
N_HEAD = 16


def draw_queries(key, part):
    fresh = jax.random.fold_in(key, 11)
    base = jnp.clip(jax.random.normal(fresh, (SEQ, TOPH, HD), jnp.float32), -6.0, 6.0)
    return base.reshape(SEQ, TOPH * HD).astype(jnp.bfloat16)


def draw_keys(key, part):
    fresh = jax.random.fold_in(key, 23)
    base = jnp.clip(jax.random.normal(fresh, (SEQ, H, HD), jnp.float32), -6.0, 6.0)
    return base.reshape(SEQ, H * HD).astype(jnp.bfloat16)


def set_ends(values, rng, low, top_value):
    shape = values.shape
    spot = [jax.random.randint(jax.random.fold_in(rng, axis), (), 0, shape[axis]) for axis in range(len(shape))]
    values = values.at[tuple(spot)].set(low)
    longest = shape.index(max(shape))
    spot[longest] = (spot[longest] + 1) % shape[longest]
    return values.at[tuple(spot)].set(top_value)


def block_levels(own_key, extent, split, smallest, high):
    def one(position, shards_of):
        steps = jax.random.uniform(jax.random.fold_in(jax.random.fold_in(own_key, 6), position), (shards_of,), jnp.float32, smallest / len(split), high / len(split))
        return jnp.repeat(jnp.exp(steps), extent[position] // shards_of).reshape((-1,) + (1,) * (len(extent) - position - 1))

    loudness = one(*split[0])
    for cut in split[1:]:
        loudness = loudness * one(*cut)
    return loudness


def deal_out(own_key, own, number, rows, count, top, reach, slope):
    order = jax.random.permutation(own_key, count)
    crowded, ordinary = portions_of(count, rows * top, reach, slope, True), portions_of(count, rows * top, reach, slope, False)
    places = jnp.arange(count)

    def named(sizes, offset_by):
        used = int((sizes > 0).sum())
        fixed = max(1, used // 4)
        passed = fixed + (places - fixed + offset_by * (used - fixed)) % max(1, count - fixed)
        return jnp.zeros((count,), jnp.int32).at[order[jnp.where(places < fixed, places, passed)]].set(jnp.asarray(sizes, jnp.int32))

    sizes = jnp.where(number % 4 == 0, named(crowded, number // 4), named(ordinary, number - number // 4 - 1))
    mixed = jax.random.permutation(jax.random.fold_in(own, 3), count)
    source_of, taker = mixed[0:count // 2 * 2:2], mixed[1:count // 2 * 2:2]
    margin = jnp.minimum(sizes[source_of] - 1, reach - sizes[taker]) // 2
    margin = jnp.where((source_of == order[0]) | (taker == order[0]) | (sizes[taker] == 0), 0, jnp.maximum(margin, 0))
    passed = jax.random.randint(jax.random.fold_in(own, 4), (count // 2,), 0, 1 << 20) % (margin + 1)
    sizes = sizes.at[source_of].add(-passed).at[taker].add(passed)
    members = jnp.searchsorted(jnp.cumsum(sizes), jnp.arange(rows * top), side="right").astype(jnp.int32)
    grid = members.reshape(top, rows).T
    grid = grid[jax.random.permutation(jax.random.fold_in(own, 1), rows)]
    offset_by = jax.random.randint(jax.random.fold_in(own, 2), (rows, 1), 0, top)
    return jnp.take_along_axis(grid, (jnp.arange(top)[None, :] + offset_by) % top, axis=1)


def portions_of(amount, total, bound, skew, full):
    weights = [(1 << 20) // math.isqrt(grade ** skew) + 1 for grade in range(1, amount + 1)]
    largest = bound if full else min(bound, max(-(-total // amount), total * weights[0] // sum(weights)))
    least = 1 if total - largest >= amount - 1 else 0
    given, rest = [largest] + [least] * (amount - 1), total - largest - least * (amount - 1)
    while rest > 0:
        free = [i for i in range(1, amount) if given[i] < largest] or [i for i in range(1, amount) if given[i] < bound]
        pool, remaining = sum([weights[i] for i in free]), rest
        for i in free:
            extra = min(bound - given[i], max(1, remaining * weights[i] // pool), rest)
            given[i] = given[i] + extra
            rest = rest - extra
    return np.array(given)


def noise(key, extent, deviation, most, split=(), kind=jnp.bfloat16):
    factor_of = block_levels(key, extent, split, -0.22, 0.18) if split else 1.0
    values = jax.random.normal(key, extent, jnp.float32) * deviation * factor_of
    return jnp.minimum(jnp.maximum(values, -most), most).astype(kind)


def setup_inputs(seed: int = 0) -> dict:
    arg_keys = jax.random.split(jax.random.key(seed), 8)
    queries = draw_queries(jax.random.fold_in(arg_keys[7], 71), 0)
    keys = draw_keys(jax.random.fold_in(arg_keys[7], 71), 0)
    values = noise(arg_keys[2], (SEQ, H * HD), 1.0, 6.0, ((0, 16), (1, 16)))
    routes_keys = jax.random.split(jax.random.fold_in(arg_keys[3], 1), SEQ // TOK_DEV)
    routes_turns = jax.random.permutation(jax.random.fold_in(arg_keys[3], 3), SEQ // TOK_DEV)
    routes = jax.vmap(lambda own, number: deal_out(jax.random.fold_in(arg_keys[3], 2), own, number, TOK_DEV, H, TOPH, CAP, 2))(routes_keys, routes_turns).reshape((SEQ, TOPH))
    gates = jnp.clip(jnp.exp(math.log(1.0) - 1.3862944 * jax.random.uniform(arg_keys[4], (SEQ, TOPH), jnp.float32) ** block_levels(arg_keys[4], (SEQ, TOPH), ((0, 256),), -0.2, 0.2)), 0.25, 1.0)
    block_mask = set_ends((jax.random.randint(arg_keys[5], (NB, NB), 0, 4) < 1).astype(jnp.int32), jax.random.fold_in(arg_keys[5], 1), 0, 1)
    w_out = noise(arg_keys[6], (H * HD, D), (TOPH * HD) ** -0.5, 0.125, ((0, 16),))
    return dict(queries=queries, keys=keys, values=values, routes=routes, gates=gates, block_mask=block_mask, w_out=w_out)


def reference(queries, keys, values, routes, gates, block_mask, w_out):
    seq_len = queries.shape[0]
    query_cube = queries.reshape(seq_len, TOPH, HD)
    key_cube = keys.reshape(seq_len, H, HD)
    value_cube = values.reshape(seq_len, H, HD)
    blocks = seq_len // BLK
    block_ids = jnp.arange(blocks, dtype=jnp.int32)
    usable = (block_ids[None, :] < block_ids[:, None]) & (block_mask == 1) | (block_ids[None, :] == block_ids[:, None])
    positions = jnp.arange(seq_len, dtype=jnp.int32)
    token_block = positions // BLK
    allowed = usable[token_block][:, token_block] & (positions[None, :] <= positions[:, None])
    score_scale = 1.0 / math.sqrt(HD)

    def one_head(head):
        chosen = routes == head
        own_query = lax.optimization_barrier(jnp.sum(jnp.where(chosen[:, :, None], query_cube.astype(jnp.float32), 0.0), axis=1)).astype(jnp.bfloat16)
        weight_sum = lax.optimization_barrier(jnp.sum(jnp.where(chosen, gates, 0.0), axis=1))
        head_keys = lax.dynamic_index_in_dim(key_cube, head, 1, keepdims=False)
        head_values = lax.dynamic_index_in_dim(value_cube, head, 1, keepdims=False)
        scores = jnp.dot(own_query, head_keys.T, preferred_element_type=jnp.float32) * score_scale
        scores = jnp.where(allowed, scores, -jnp.inf)
        peak = lax.optimization_barrier(jnp.max(scores, axis=1, keepdims=True))
        weights = jnp.exp(scores - peak)
        total = lax.optimization_barrier(jnp.sum(weights, axis=1, keepdims=True))
        mixed = jnp.dot(weights.astype(jnp.bfloat16), head_values, preferred_element_type=jnp.float32) / total
        return (mixed * weight_sum[:, None]).astype(jnp.bfloat16)
    heads_out = lax.map(one_head, jnp.arange(H, dtype=jnp.int32))
    weighted = heads_out.transpose(1, 0, 2).reshape(seq_len, H * HD)
    group = H // N_HEAD * HD

    def add_group(index, running):
        columns = lax.dynamic_slice_in_dim(weighted, index * group, group, 1)
        row_block = lax.dynamic_slice_in_dim(w_out, index * group, group, 0)
        term = jnp.dot(columns, row_block, preferred_element_type=jnp.float32)
        term = lax.optimization_barrier(term.astype(jnp.bfloat16)).astype(jnp.float32)
        return running + term
    summed = lax.fori_loop(0, N_HEAD, add_group, jnp.zeros((seq_len, D), jnp.float32))
    return summed.astype(jnp.bfloat16)
```

```python
import math

import jax
import jax.numpy as jnp
from jax import lax
from jax.experimental import pallas as pl
from jax.experimental.pallas import tpu as pltpu
from jax.sharding import PartitionSpec as P

H = 64
HD = 128
BLK = 128
CAP = 16
NX = 4
NJ = 4
NZ = 8
HALF = 2048
NEG = -1e30
SCALE2 = math.log2(math.e) / math.sqrt(HD)
BF = jnp.bfloat16
F32 = jnp.float32
NT = (((1,), (1,)), ((), ()))


def vmem():
    return pl.BlockSpec(memory_space=pltpu.VMEM)


def grant(mib):
    return pltpu.CompilerParams(vmem_limit_bytes=mib << 20)


def pack_kernel(q_ref, tgt_ref, gate_ref, out_ref):
    rows = jnp.concatenate([q_ref[:, k * HD : (k + 1) * HD] for k in range(16)], axis=0)
    tgt = tgt_ref[...]
    gate = gate_ref[...]
    hi = gate.astype(BF).astype(F32)
    mid = (gate - hi).astype(BF).astype(F32)
    tok = (lax.broadcasted_iota(jnp.int32, (1, 512), 1) % 32 + 1).astype(F32)
    aux = jnp.concatenate([tok, hi, mid, gate - hi - mid, jnp.zeros((12, 512), F32)], axis=0).astype(BF)
    for dest in range(16):
        slot = lax.broadcasted_iota(jnp.int32, (64, 512), 0) + dest * 64
        sel = jnp.where(slot == tgt, 1.0, 0.0).astype(BF)
        out_ref[dest, 0:64, :] = jnp.dot(sel, rows, preferred_element_type=F32).astype(BF)
        meta = lax.dot_general(aux, sel, NT, preferred_element_type=F32)
        meta = jnp.concatenate([meta, jnp.zeros((16, 64), F32)], axis=1)
        out_ref[dest, 64:80, :] = meta.astype(BF)


def attend_kernel(sets, flag_ref, bias_ref, lim_ref, *refs):
    count = len(sets)
    q_refs, kv_refs, out_refs = refs[:count], refs[count : count + 4], refs[count + 4 : 2 * count + 4]
    kv, sems, list_ref, done_ref, s_ref, m_ref, acc_ref = refs[2 * count + 4 :]
    copies = [pltpu.make_async_copy(src, kv.at[i], sems.at[i]) for i, src in enumerate(kv_refs)]
    for copy in copies:
        copy.start()
    copies[0].wait()
    done_ref[0] = jnp.int32(0)

    def keys_ready(last):
        for i in range(1, 4):

            @pl.when((last >= i) & (done_ref[0] < i))
            def _():
                copies[i].wait()
                done_ref[0] = jnp.int32(i)

    ones = jnp.ones((16, 256), BF)
    key_id = lax.broadcasted_iota(jnp.int32, (BLK, 256), 0).astype(F32)

    def two_blocks(q_ref, first, second, bias, lims):
        blocks = (first, second)
        state = {}

        def scores(p):
            q = q_ref[:, p * CAP : (p + 1) * CAP, :].reshape(256, HD)
            old = m_ref[p : p + 1, :]
            new = old
            for n, block in enumerate(blocks):
                k = kv[block // 4, pl.ds(pl.multiple_of((block % 4) * BLK, BLK), BLK), p * HD : (p + 1) * HD]
                s = lax.dot_general(k, q, NT, preferred_element_type=F32)
                if lims is not None:
                    s = jnp.where(key_id <= lims(p, n), s, 2.0 * NEG)
                s_ref[p, n * BLK : (n + 1) * BLK, :] = s
                top = jnp.max(s, axis=0, keepdims=True)
                new = jnp.maximum(new, top if bias is None else top + bias[n])
            m_ref[p : p + 1, :] = new
            state[p] = (new, jnp.exp2((old - new) * SCALE2))

        def values(p):
            new, factor = state[p]
            ws, vts = [], []
            for n, block in enumerate(blocks):
                base = new if bias is None else new - bias[n]
                ws.append(jnp.exp2((s_ref[p, n * BLK : (n + 1) * BLK, :] - base) * SCALE2).astype(BF))
                vts.append(kv[block // 4, 512 + p * HD : 512 + (p + 1) * HD, pl.ds(pl.multiple_of((block % 4) * BLK, BLK), BLK)])
            left = jnp.concatenate([jnp.concatenate(vts, axis=1), ones], axis=0)
            gain = jnp.dot(left, jnp.concatenate(ws, axis=0), preferred_element_type=F32)
            acc_ref[p * 144 : (p + 1) * 144, :] = acc_ref[p * 144 : (p + 1) * 144, :] * factor + gain

        scores(0)
        scores(1)
        values(0)
        scores(2)
        values(1)
        scores(3)
        values(2)
        values(3)

    for n, dx in enumerate(sets):
        q_ref, out_ref = q_refs[n], out_refs[n]
        m_ref[...] = jnp.full(m_ref.shape, NEG, F32)
        acc_ref[...] = jnp.zeros(acc_ref.shape, F32)
        if dx == 0:

            def diag_step(pair, _, q_ref=q_ref):
                def lims(p, n):
                    return lim_ref[pl.ds(p * 4 + pair * 2 + n, 1), :]

                two_blocks(q_ref, pair * 2, pair * 2 + 1, None, lims)
                return 0

            lax.fori_loop(0, 2, diag_step, 0)
        found = jnp.int32(0)
        for block in range(4 if dx == 0 else 0, 16):
            list_ref[found] = jnp.int32(block)
            found = found + flag_ref[dx, block]
        list_ref[found] = jnp.int32(16)

        def pair_step(pair, _, q_ref=q_ref, dx=dx, n=n):
            one, two = list_ref[pair * 2], list_ref[pair * 2 + 1]
            if n == 0:
                keys_ready(jnp.minimum(two, 15) // 4)
            bias = (bias_ref[pl.ds(dx * 24 + one, 1), :], bias_ref[pl.ds(dx * 24 + two, 1), :])
            two_blocks(q_ref, one, jnp.minimum(two, 15), bias, None)
            return 0

        lax.fori_loop(0, (found + 1) // 2, pair_step, 0)
        if n == 0:
            keys_ready(3)
        total = jnp.concatenate([acc_ref[p * 144 + HD : p * 144 + HD + 1, :] for p in range(4)], axis=0)
        some = total > 0.0
        safe = jnp.where(some, total, 1.0)
        inv = jnp.where(some, 1.0 / safe, 0.0)
        lse = jnp.where(some, m_ref[0:4, :] * SCALE2 + jnp.log2(safe), NEG)
        hi = lse.astype(BF)
        rest = lse - hi.astype(F32)
        mid = rest.astype(BF)
        low = (rest - mid.astype(F32)).astype(BF)
        for p in range(4):
            out_ref[p * HD : (p + 1) * HD, :] = (acc_ref[p * 144 : p * 144 + HD, :] * inv[p : p + 1, :]).astype(BF)
        out_ref[512:528, :] = jnp.concatenate([hi, mid, low, jnp.zeros((4, 256), BF)], axis=0)


def attend(sets, flags, bias, lim, qs, kvs):
    part = jax.ShapeDtypeStruct((528, 256), BF)
    return pl.pallas_call(
        lambda *refs: attend_kernel(sets, *refs),
        out_shape=[part] * len(sets),
        in_specs=[pl.BlockSpec(memory_space=pltpu.SMEM)]
        + [vmem()] * (2 + len(sets))
        + [pl.BlockSpec(memory_space=pl.ANY)] * 4,
        out_specs=[vmem()] * len(sets),
        scratch_shapes=[
            pltpu.VMEM((4, 1024, 512), BF),
            pltpu.SemaphoreType.DMA((4,)),
            pltpu.SMEM((18,), jnp.int32),
            pltpu.SMEM((1,), jnp.int32),
            pltpu.VMEM((4, 256, 256), F32),
            pltpu.VMEM((8, 256), F32),
            pltpu.VMEM((576, 256), F32),
        ],
        cost_estimate=pl.CostEstimate(
            flops=len(sets) * 2 * 2 * 4 * 256 * 2048 * 128,
            bytes_accessed=5 << 20,
            transcendentals=len(sets) * 4 * 256 * 2048,
        ),
        compiler_params=grant(24),
        name="attend",
    )(flags, bias, lim, *qs, *kvs)


def place_heads(heads, pos, out_ref, lo):
    token = lax.broadcasted_iota(jnp.int32, (256, HD), 0).astype(F32)
    for r in range(2):
        place = jnp.where(token + r * 256.0 == pos[:, r * HD : (r + 1) * HD], 1.0, 0.0).astype(BF)
        out_ref[r * 256 : (r + 1) * 256, lo : lo + HD] = lax.dot_general(
            place, heads[:, r * HD : (r + 1) * HD], NT, preferred_element_type=F32
        ).astype(BF)


def slot_pos(tok):
    dev = (lax.broadcasted_iota(jnp.int32, tok.shape, 1) // CAP).astype(F32)
    return jnp.where(tok >= 0.0, dev * 32.0 + tok, -1.0)


def merge_kernel(a_ref, b_ref, c_ref, d_ref, tok_ref, gate_ref, send_ref):
    parts = (a_ref, b_ref, c_ref, d_ref)
    lses = []
    for ref in parts:
        tail = ref[512:528, :].astype(F32)
        lses.append(tail[0:4] + tail[4:8] + tail[8:12])
    top = jnp.maximum(jnp.maximum(lses[0], lses[1]), jnp.maximum(lses[2], lses[3]))
    ws = [jnp.exp2(lse - top) for lse in lses]
    norm = gate_ref[...] / (ws[0] + ws[1] + ws[2] + ws[3])
    ws = [w * norm for w in ws]
    for p in range(4):
        mix = None
        for ref, w in zip(parts, ws):
            term = ref[p * HD : (p + 1) * HD, :].astype(F32) * w[p : p + 1, :]
            mix = term if mix is None else mix + term
        send_ref[p * HD : (p + 1) * HD, :] = mix.astype(BF)
    send_ref[512:528, :] = jnp.concatenate([tok_ref[...], jnp.zeros((12, 256), F32)], axis=0).astype(BF)


def own_kernel(place_ref, sent_ref, w_ref, out_ref, a_ref):
    @pl.when(pl.program_id(0) == 0)
    def _():
        pos = slot_pos(sent_ref[512:528, :].astype(F32))
        for p in range(4):
            place_heads(sent_ref[p * HD : (p + 1) * HD, :], pos[p : p + 1, :], a_ref, p * HD)

    out_ref[...] = jnp.dot(a_ref[...], w_ref[...], preferred_element_type=F32).astype(BF)


def partner_kernel(place_ref, got_ref, own_ref, wb_ref, wc_ref, out_ref, plus_ref, minus_ref, a_ref):
    @pl.when(pl.program_id(0) == 0)
    def _():
        pos = slot_pos(got_ref[512:528, :].astype(F32))
        core = place_ref[1]
        for n in range(4):
            half = core if n < 2 else 1 - core
            q = n % 2
            start = pl.multiple_of(half * 256 + q * HD, HD)
            row = jnp.where(half == 0, pos[q : q + 1, :], pos[2 + q : 3 + q, :])
            place_heads(got_ref[pl.ds(start, HD), :], row, a_ref, n * HD)

    total = own_ref[...].astype(F32)
    total += jnp.dot(a_ref[:, 0:256], wb_ref[...], preferred_element_type=F32)
    total += jnp.dot(a_ref[:, 256:512], wc_ref[...], preferred_element_type=F32)
    out_ref[...] = total.astype(BF)
    for ref, dest in ((plus_ref, place_ref[2]), (minus_ref, place_ref[3])):
        for half in range(2):
            ref[half] = out_ref[pl.ds(pl.multiple_of(half * 256 + dest * 32, 32), 32), :]


TILE = 512
STEPS = HALF // TILE


def own_product(place, sent, w_out):
    return pl.pallas_call(
        own_kernel,
        out_shape=jax.ShapeDtypeStruct((512, 2 * HALF), BF),
        grid_spec=pltpu.PrefetchScalarGridSpec(
            num_scalar_prefetch=1,
            grid=(2 * STEPS,),
            in_specs=[
                pl.BlockSpec((528, 256), lambda i, s: (0, 0)),
                pl.BlockSpec((512, TILE), lambda i, s: (0, s[0] * (2 * STEPS) + i)),
            ],
            out_specs=pl.BlockSpec((512, TILE), lambda i, s: (0, i)),
            scratch_shapes=[pltpu.VMEM((512, 512), BF)],
        ),
        cost_estimate=pl.CostEstimate(flops=2 * 512 * 512 * 2 * HALF, bytes_accessed=8 << 20, transcendentals=0),
        name="own_product",
    )(place, sent, w_out)


def with_partner(place, chunk, got, own, wb, wc):
    message = jax.ShapeDtypeStruct((2, 32, HALF), BF)
    return pl.pallas_call(
        partner_kernel,
        out_shape=[jax.ShapeDtypeStruct((512, HALF), BF), message, message],
        grid_spec=pltpu.PrefetchScalarGridSpec(
            num_scalar_prefetch=1,
            grid=(STEPS,),
            in_specs=[
                pl.BlockSpec((528, 256), lambda i, s: (0, 0)),
                pl.BlockSpec((512, TILE), lambda i, s: (0, chunk * STEPS + i)),
                pl.BlockSpec((256, TILE), lambda i, s: (0, i)),
                pl.BlockSpec((256, TILE), lambda i, s: (0, i)),
            ],
            out_specs=[pl.BlockSpec((512, TILE), lambda i, s: (0, i))]
            + [pl.BlockSpec((2, 32, TILE), lambda i, s: (0, 0, i))] * 2,
            scratch_shapes=[pltpu.VMEM((512, 512), BF)],
        ),
        cost_estimate=pl.CostEstimate(flops=2 * 512 * 512 * HALF, bytes_accessed=6 << 20, transcendentals=0),
        name="with_partner",
    )(place, got, own, wb, wc)


def layer(queries, keys, values, routes, gates, block_mask, w_out):
    ctx = lax.axis_index("ctx")
    head = lax.axis_index("head")
    x, j = ctx // NJ, ctx % NJ
    y, z = head // NZ, head % NZ

    def move_ctx(v, f):
        return lax.ppermute(v, "ctx", [(i, f(i)) for i in range(16)])

    def move_head(v, f):
        return lax.ppermute(v, "head", [(i, f(i)) for i in range(16)])

    def swap(i):
        return i ^ NZ

    given = lax.dynamic_slice(w_out, ((ctx % 2) * 256, (1 - y) * 2 * HALF), (256, 2 * HALF))
    w_fetched = [move_head(given[:, n * HALF : (n + 1) * HALF], swap) for n in range(2)]

    kv = jnp.concatenate([keys, values.T], axis=0)
    kv2 = move_ctx(kv, lambda i: i ^ 2)
    kv1 = move_ctx(kv, lambda i: i ^ 1)

    head_ids = jnp.arange(H, dtype=jnp.int32)
    onehot = (routes[:, :, None] == head_ids[None, None, :]).astype(F32)
    per_token = jnp.sum(onehot, axis=1)
    below = (jnp.arange(32)[:, None] > jnp.arange(32)[None, :]).astype(F32)
    earlier = jnp.dot(below, per_token, preferred_element_type=F32)
    ranking = jnp.sum(onehot * earlier[:, None, :], axis=2).astype(jnp.int32)
    target = (routes * CAP + ranking).T.reshape(1, 512)
    gate_row = gates.T.reshape(1, 512)
    packed = pl.pallas_call(
        pack_kernel,
        out_shape=jax.ShapeDtypeStruct((16, 80, HD), BF),
        in_specs=[vmem()] * 3,
        out_specs=vmem(),
        compiler_params=grant(12),
        name="pack",
    )(queries, target, gate_row)
    arrived = lax.all_to_all(packed, "head", split_axis=0, concat_axis=0, tiled=True)
    q_own = arrived[:, :64, :]
    meta = arrived[:, 64:68, :64].astype(F32).reshape(16, 4, 4, CAP).transpose(1, 2, 0, 3).reshape(4, 4, 256)
    tok = meta[0] - 1.0
    gate = meta[1] + meta[2] + meta[3]
    dev = (jnp.arange(256) // CAP).astype(F32)
    in_block = jnp.maximum(tok, 0.0) + (dev[None, :] % 4.0) * 32.0

    a_id = jnp.arange(64)
    usable = (block_mask == 1) & (a_id[None, :] < a_id[:, None])
    usable = lax.dynamic_index_in_dim(usable.reshape(NX, NJ, 4, NX, NJ, 4), j, 1, keepdims=False)
    usable = lax.dynamic_index_in_dim(usable, x, 2, keepdims=False)
    usable = jnp.stack([lax.dynamic_index_in_dim(usable, j ^ i, 2, keepdims=False) for i in range(4)], axis=2)
    usable = jnp.stack([lax.dynamic_index_in_dim(usable, (x + dx) % NX, 0, keepdims=False) for dx in range(4)])
    flags = jnp.any(usable, axis=1).astype(jnp.int32).reshape(4, 16)
    bias = jnp.where(usable, 0.0, 2.0 * NEG).reshape(4, 4, 16).transpose(0, 2, 1)
    bias = jnp.concatenate([bias, jnp.full((4, 8, 4), 2.0 * NEG, F32)], axis=1)
    bias = jnp.repeat(bias, 64, axis=2).reshape(96, 256)
    same = (jnp.arange(256)[None, :] // 64) == jnp.arange(4)[:, None]
    earlier_ok = jnp.where(bias[0:4] == 0.0, 127.0, -1.0)
    lim = jnp.where(same[None], in_block[:, None, :], earlier_ok[None]).reshape(16, 256)

    q1 = move_ctx(q_own, lambda i: (i - 4) % 16)
    q2 = move_ctx(q_own, lambda i: (i - 8) % 16)
    q3 = move_ctx(q_own, lambda i: (i - 12) % 16)
    kv3 = move_ctx(kv2, lambda i: i ^ 1)
    kvs = (kv, kv1, kv2, kv3)
    parts = attend((1, 2, 3), flags, bias, lim, (q1, q2, q3), kvs)
    back = [move_ctx(part, lambda i: (i + 4 * dx) % 16) for dx, part in ((1, parts[0]), (2, parts[1]), (3, parts[2]))]
    (own,) = attend((0,), flags, bias, lim, (q_own,), kvs)
    sent = pl.pallas_call(
        merge_kernel,
        out_shape=jax.ShapeDtypeStruct((528, 256), BF),
        in_specs=[vmem()] * 6,
        out_specs=vmem(),
        compiler_params=grant(8),
        name="merge",
    )(own, *back, tok, gate)
    got = move_head(sent, swap)
    w_swapped = [move_ctx(w, lambda i: i ^ 1) for w in w_fetched]
    mine = own_product(jnp.stack([y, ctx % 2]), sent, w_out)

    def shift(step):
        return lambda i: (i // NZ) * NZ + (i % NZ + step) % NZ

    here, there = [], []
    for chunk, hops in ((0, (4, 3)), (1, (3, 4))):
        where = jnp.stack([y, ctx % 2, (z + hops[0]) % NZ, (z - hops[1]) % NZ])
        product, *first = with_partner(where, chunk, got, mine, w_fetched[chunk], w_swapped[chunk])
        product = product.reshape(2, NZ, 32, HALF)

        def term(dest, product=product):
            return lax.dynamic_index_in_dim(product, dest % NZ, 1, keepdims=False)

        total = term(z).astype(F32)
        for step, length, message in zip((1, -1), hops, first):
            for hop in range(length):
                if hop:
                    message = (message.astype(F32) + term(z + step * (length - hop)).astype(F32)).astype(BF)
                message = move_head(message, shift(step))
            total = total + message.astype(F32)
        total = total.astype(BF)
        here.append(lax.dynamic_index_in_dim(total, y, 0, keepdims=False))
        there.append(move_head(lax.dynamic_index_in_dim(total, 1 - y, 0, keepdims=False), swap))
    low = [jnp.where(y == 0, h, t) for h, t in zip(here, there)]
    high = [jnp.where(y == 0, t, h) for h, t in zip(here, there)]
    return jnp.concatenate(low + high, axis=1)


def solution(mesh):
    placed = (
        P(("ctx", "head"), None),
        P("ctx", "head"),
        P("ctx", "head"),
        P(("ctx", "head"), None),
        P(("ctx", "head"), None),
        P(),
        P("head", None),
    )
    return jax.shard_map(layer, mesh=mesh, in_specs=placed, out_specs=P(("ctx", "head"), None), check_vma=False)
```

```python
import math

import jax
import jax.numpy as jnp
from jax import lax
from jax.experimental import pallas as pl
from jax.experimental.pallas import tpu as pltpu
from jax.sharding import PartitionSpec as P

H = 64
HD = 128
BLK = 128
CAP = 16
NX = 4
NJ = 4
NZ = 8
HALF = 2048
NEG = -1e30
SCALE2 = math.log2(math.e) / math.sqrt(HD)
BF = jnp.bfloat16
F32 = jnp.float32
NT = (((1,), (1,)), ((), ()))


def vmem():
    return pl.BlockSpec(memory_space=pltpu.VMEM)


def grant(mib):
    return pltpu.CompilerParams(vmem_limit_bytes=mib << 20)


def pack_kernel(q_ref, tgt_ref, gate_ref, out_ref):
    rows = jnp.concatenate([q_ref[:, k * HD : (k + 1) * HD] for k in range(16)], axis=0)
    tgt = tgt_ref[...]
    gate = gate_ref[...]
    hi = gate.astype(BF).astype(F32)
    mid = (gate - hi).astype(BF).astype(F32)
    tok = (lax.broadcasted_iota(jnp.int32, (1, 512), 1) % 32 + 1).astype(F32)
    aux = jnp.concatenate([tok, hi, mid, gate - hi - mid, jnp.zeros((12, 512), F32)], axis=0).astype(BF)
    for dest in range(16):
        slot = lax.broadcasted_iota(jnp.int32, (64, 512), 0) + dest * 64
        sel = jnp.where(slot == tgt, 1.0, 0.0).astype(BF)
        out_ref[dest, 0:64, :] = jnp.dot(sel, rows, preferred_element_type=F32).astype(BF)
        meta = lax.dot_general(aux, sel, NT, preferred_element_type=F32)
        meta = jnp.concatenate([meta, jnp.zeros((16, 64), F32)], axis=1)
        out_ref[dest, 64:80, :] = meta.astype(BF)


def attend_kernel(sets, flag_ref, bias_ref, lim_ref, *refs):
    count = len(sets)
    q_refs, kv_refs, out_refs = refs[:count], refs[count : count + 4], refs[count + 4 : 2 * count + 4]
    kv, sems, list_ref, done_ref, s_ref, m_ref, acc_ref = refs[2 * count + 4 :]
    copies = [pltpu.make_async_copy(src, kv.at[i], sems.at[i]) for i, src in enumerate(kv_refs)]
    for copy in copies:
        copy.start()
    copies[0].wait()
    done_ref[0] = jnp.int32(0)

    def keys_ready(last):
        for i in range(1, 4):

            @pl.when((last >= i) & (done_ref[0] < i))
            def _():
                copies[i].wait()
                done_ref[0] = jnp.int32(i)

    ones = jnp.ones((16, 256), BF)
    key_id = lax.broadcasted_iota(jnp.int32, (BLK, 256), 0).astype(F32)

    def two_blocks(q_ref, first, second, bias, lims):
        blocks = (first, second)
        state = {}

        def scores(p):
            q = q_ref[:, p * CAP : (p + 1) * CAP, :].reshape(256, HD)
            old = m_ref[p : p + 1, :]
            new = old
            for n, block in enumerate(blocks):
                k = kv[block // 4, pl.ds(pl.multiple_of((block % 4) * BLK, BLK), BLK), p * HD : (p + 1) * HD]
                s = lax.dot_general(k, q, NT, preferred_element_type=F32)
                if lims is not None:
                    s = jnp.where(key_id <= lims(p, n), s, 2.0 * NEG)
                s_ref[p, n * BLK : (n + 1) * BLK, :] = s
                top = jnp.max(s, axis=0, keepdims=True)
                new = jnp.maximum(new, top if bias is None else top + bias[n])
            m_ref[p : p + 1, :] = new
            state[p] = (new, jnp.exp2((old - new) * SCALE2))

        def values(p):
            new, factor = state[p]
            ws, vts = [], []
            for n, block in enumerate(blocks):
                base = new if bias is None else new - bias[n]
                ws.append(jnp.exp2((s_ref[p, n * BLK : (n + 1) * BLK, :] - base) * SCALE2).astype(BF))
                vts.append(kv[block // 4, 512 + p * HD : 512 + (p + 1) * HD, pl.ds(pl.multiple_of((block % 4) * BLK, BLK), BLK)])
            left = jnp.concatenate([jnp.concatenate(vts, axis=1), ones], axis=0)
            gain = jnp.dot(left, jnp.concatenate(ws, axis=0), preferred_element_type=F32)
            acc_ref[p * 144 : (p + 1) * 144, :] = acc_ref[p * 144 : (p + 1) * 144, :] * factor + gain

        scores(0)
        scores(1)
        values(0)
        scores(2)
        values(1)
        scores(3)
        values(2)
        values(3)

    for n, dx in enumerate(sets):
        q_ref, out_ref = q_refs[n], out_refs[n]
        m_ref[...] = jnp.full(m_ref.shape, NEG, F32)
        acc_ref[...] = jnp.zeros(acc_ref.shape, F32)
        if dx == 0:

            def diag_step(pair, _, q_ref=q_ref):
                def lims(p, n):
                    return lim_ref[pl.ds(p * 4 + pair * 2 + n, 1), :]

                two_blocks(q_ref, pair * 2, pair * 2 + 1, None, lims)
                return 0

            lax.fori_loop(0, 2, diag_step, 0)
        found = jnp.int32(0)
        for block in range(4 if dx == 0 else 0, 16):
            list_ref[found] = jnp.int32(block)
            found = found + flag_ref[dx, block]
        list_ref[found] = jnp.int32(16)

        def pair_step(pair, _, q_ref=q_ref, dx=dx, n=n):
            one, two = list_ref[pair * 2], list_ref[pair * 2 + 1]
            if n == 0:
                keys_ready(jnp.minimum(two, 15) // 4)
            bias = (bias_ref[pl.ds(dx * 24 + one, 1), :], bias_ref[pl.ds(dx * 24 + two, 1), :])
            two_blocks(q_ref, one, jnp.minimum(two, 15), bias, None)
            return 0

        lax.fori_loop(0, (found + 1) // 2, pair_step, 0)
        if n == 0:
            keys_ready(3)
        total = jnp.concatenate([acc_ref[p * 144 + HD : p * 144 + HD + 1, :] for p in range(4)], axis=0)
        some = total > 0.0
        safe = jnp.where(some, total, 1.0)
        inv = jnp.where(some, 1.0 / safe, 0.0)
        lse = jnp.where(some, m_ref[0:4, :] * SCALE2 + jnp.log2(safe), NEG)
        hi = lse.astype(BF)
        rest = lse - hi.astype(F32)
        mid = rest.astype(BF)
        low = (rest - mid.astype(F32)).astype(BF)
        for p in range(4):
            out_ref[p * HD : (p + 1) * HD, :] = (acc_ref[p * 144 : p * 144 + HD, :] * inv[p : p + 1, :]).astype(BF)
        out_ref[512:528, :] = jnp.concatenate([hi, mid, low, jnp.zeros((4, 256), BF)], axis=0)


def attend(sets, flags, bias, lim, qs, kvs):
    part = jax.ShapeDtypeStruct((528, 256), BF)
    return pl.pallas_call(
        lambda *refs: attend_kernel(sets, *refs),
        out_shape=[part] * len(sets),
        in_specs=[pl.BlockSpec(memory_space=pltpu.SMEM)]
        + [vmem()] * (2 + len(sets))
        + [pl.BlockSpec(memory_space=pl.ANY)] * 4,
        out_specs=[vmem()] * len(sets),
        scratch_shapes=[
            pltpu.VMEM((4, 1024, 512), BF),
            pltpu.SemaphoreType.DMA((4,)),
            pltpu.SMEM((18,), jnp.int32),
            pltpu.SMEM((1,), jnp.int32),
            pltpu.VMEM((4, 256, 256), F32),
            pltpu.VMEM((8, 256), F32),
            pltpu.VMEM((576, 256), F32),
        ],
        cost_estimate=pl.CostEstimate(
            flops=len(sets) * 2 * 2 * 4 * 256 * 2048 * 128,
            bytes_accessed=5 << 20,
            transcendentals=len(sets) * 4 * 256 * 2048,
        ),
        compiler_params=grant(24),
        name="attend",
    )(flags, bias, lim, *qs, *kvs)


def place_heads(heads, pos, out_ref, lo):
    token = lax.broadcasted_iota(jnp.int32, (256, HD), 0).astype(F32)
    for r in range(2):
        place = jnp.where(token + r * 256.0 == pos[:, r * HD : (r + 1) * HD], 1.0, 0.0).astype(BF)
        out_ref[r * 256 : (r + 1) * 256, lo : lo + HD] = lax.dot_general(
            place, heads[:, r * HD : (r + 1) * HD], NT, preferred_element_type=F32
        ).astype(BF)


def slot_pos(tok):
    dev = (lax.broadcasted_iota(jnp.int32, tok.shape, 1) // CAP).astype(F32)
    return jnp.where(tok >= 0.0, dev * 32.0 + tok, -1.0)


def merge_kernel(a_ref, b_ref, c_ref, d_ref, tok_ref, gate_ref, send_ref):
    parts = (a_ref, b_ref, c_ref, d_ref)
    lses = []
    for ref in parts:
        tail = ref[512:528, :].astype(F32)
        lses.append(tail[0:4] + tail[4:8] + tail[8:12])
    top = jnp.maximum(jnp.maximum(lses[0], lses[1]), jnp.maximum(lses[2], lses[3]))
    ws = [jnp.exp2(lse - top) for lse in lses]
    norm = gate_ref[...] / (ws[0] + ws[1] + ws[2] + ws[3])
    ws = [w * norm for w in ws]
    for p in range(4):
        mix = None
        for ref, w in zip(parts, ws):
            term = ref[p * HD : (p + 1) * HD, :].astype(F32) * w[p : p + 1, :]
            mix = term if mix is None else mix + term
        send_ref[p * HD : (p + 1) * HD, :] = mix.astype(BF)
    send_ref[512:528, :] = jnp.concatenate([tok_ref[...], jnp.zeros((12, 256), F32)], axis=0).astype(BF)


def place_kernel(sent_ref, out_ref):
    pos = slot_pos(sent_ref[512:528, :].astype(F32))
    for p in range(4):
        place_heads(sent_ref[p * HD : (p + 1) * HD, :], pos[p : p + 1, :], out_ref, p * HD)


def spread_kernel(core_ref, got_ref, out_ref):
    pos = slot_pos(got_ref[512:528, :].astype(F32))
    core = core_ref[0]
    for n in range(4):
        half = core if n < 2 else 1 - core
        q = n % 2
        start = pl.multiple_of(half * 256 + q * HD, HD)
        row = jnp.where(half == 0, pos[q : q + 1, :], pos[2 + q : 3 + q, :])
        place_heads(got_ref[pl.ds(start, HD), :], row, out_ref, n * HD)


def project_kernel(hops, place_ref, a_ref, b_ref, wa_ref, wb_ref, wc_ref, up0_ref, up_ref, down0_ref, down_ref, own_ref, total_ref):
    total = jnp.dot(a_ref[...], wa_ref[...], preferred_element_type=F32)
    total += jnp.dot(b_ref[:, 0:256], wb_ref[...], preferred_element_type=F32)
    total += jnp.dot(b_ref[:, 256:512], wc_ref[...], preferred_element_type=F32)
    total_ref[...] = total.astype(BF)
    z = place_ref[1]

    def rows(half, ahead):
        dest = (z + (ahead + NZ)) % NZ
        return total_ref[pl.ds(pl.multiple_of(half * 256 + dest * 32, 32), 32), :]

    for half in range(2):
        own_ref[half] = rows(half, 0)
        for step, length, first, rest in ((1, hops[0], up0_ref, up_ref), (-1, hops[1], down0_ref, down_ref)):
            first[half] = rows(half, step * length)
            for hop in range(1, length):
                rest[hop - 1, half] = rows(half, step * (length - hop))


TILE = 512
STEPS = HALF // TILE


def project(place, chunk, hops, a, b, w_out, wb, wc):
    def terms(*lead):
        return jax.ShapeDtypeStruct((*lead, 2, 32, HALF), BF)

    def block(*lead):
        zeros = (0,) * (len(lead) + 2)
        return pl.BlockSpec((*lead, 2, 32, TILE), lambda i, s: (*zeros, i))

    leads = ((), (hops[0] - 1,), (), (hops[1] - 1,), ())
    return pl.pallas_call(
        lambda *refs: project_kernel(hops, *refs),
        out_shape=[terms(*lead) for lead in leads],
        grid_spec=pltpu.PrefetchScalarGridSpec(
            num_scalar_prefetch=1,
            grid=(STEPS,),
            in_specs=[
                pl.BlockSpec((512, 512), lambda i, s: (0, 0)),
                pl.BlockSpec((512, 512), lambda i, s: (0, 0)),
                pl.BlockSpec((512, TILE), lambda i, s: (0, s[0] * (2 * STEPS) + chunk * STEPS + i)),
                pl.BlockSpec((256, TILE), lambda i, s: (0, i)),
                pl.BlockSpec((256, TILE), lambda i, s: (0, i)),
            ],
            out_specs=[block(*lead) for lead in leads],
            scratch_shapes=[pltpu.VMEM((512, TILE), BF)],
        ),
        cost_estimate=pl.CostEstimate(flops=2 * 512 * 1024 * HALF, bytes_accessed=7 << 20, transcendentals=0),
        name="project",
    )(place, a, b, w_out, wb, wc)


def layer(queries, keys, values, routes, gates, block_mask, w_out):
    ctx = lax.axis_index("ctx")
    head = lax.axis_index("head")
    x, j = ctx // NJ, ctx % NJ
    y, z = head // NZ, head % NZ

    def move_ctx(v, f):
        return lax.ppermute(v, "ctx", [(i, f(i)) for i in range(16)])

    def move_head(v, f):
        return lax.ppermute(v, "head", [(i, f(i)) for i in range(16)])

    def swap(i):
        return i ^ NZ

    w_fetched = []
    for n in range(2):
        given = lax.dynamic_slice(w_out, ((ctx % 2) * 256, (2 * (1 - y) + n) * HALF), (256, HALF))
        w_fetched.append(move_head(given, swap))

    kv = jnp.concatenate([keys, values.T], axis=0)
    kv2 = move_ctx(kv, lambda i: i ^ 2)
    kv1 = move_ctx(kv, lambda i: i ^ 1)

    head_ids = jnp.arange(H, dtype=jnp.int32)
    onehot = (routes[:, :, None] == head_ids[None, None, :]).astype(F32)
    per_token = jnp.sum(onehot, axis=1)
    below = (jnp.arange(32)[:, None] > jnp.arange(32)[None, :]).astype(F32)
    earlier = jnp.dot(below, per_token, preferred_element_type=F32)
    ranking = jnp.sum(onehot * earlier[:, None, :], axis=2).astype(jnp.int32)
    target = (routes * CAP + ranking).T.reshape(1, 512)
    gate_row = gates.T.reshape(1, 512)
    packed = pl.pallas_call(
        pack_kernel,
        out_shape=jax.ShapeDtypeStruct((16, 80, HD), BF),
        in_specs=[vmem()] * 3,
        out_specs=vmem(),
        compiler_params=grant(12),
        name="pack",
    )(queries, target, gate_row)
    arrived = lax.all_to_all(packed, "head", split_axis=0, concat_axis=0, tiled=True)
    q_own = arrived[:, :64, :]
    meta = arrived[:, 64:68, :64].astype(F32).reshape(16, 4, 4, CAP).transpose(1, 2, 0, 3).reshape(4, 4, 256)
    tok = meta[0] - 1.0
    gate = meta[1] + meta[2] + meta[3]
    dev = (jnp.arange(256) // CAP).astype(F32)
    in_block = jnp.maximum(tok, 0.0) + (dev[None, :] % 4.0) * 32.0

    a_id = jnp.arange(64)
    usable = (block_mask == 1) & (a_id[None, :] < a_id[:, None])
    usable = lax.dynamic_index_in_dim(usable.reshape(NX, NJ, 4, NX, NJ, 4), j, 1, keepdims=False)
    usable = lax.dynamic_index_in_dim(usable, x, 2, keepdims=False)
    usable = jnp.stack([lax.dynamic_index_in_dim(usable, j ^ i, 2, keepdims=False) for i in range(4)], axis=2)
    usable = jnp.stack([lax.dynamic_index_in_dim(usable, (x + dx) % NX, 0, keepdims=False) for dx in range(4)])
    flags = jnp.any(usable, axis=1).astype(jnp.int32).reshape(4, 16)
    bias = jnp.where(usable, 0.0, 2.0 * NEG).reshape(4, 4, 16).transpose(0, 2, 1)
    bias = jnp.concatenate([bias, jnp.full((4, 8, 4), 2.0 * NEG, F32)], axis=1)
    bias = jnp.repeat(bias, 64, axis=2).reshape(96, 256)
    same = (jnp.arange(256)[None, :] // 64) == jnp.arange(4)[:, None]
    earlier_ok = jnp.where(bias[0:4] == 0.0, 127.0, -1.0)
    lim = jnp.where(same[None], in_block[:, None, :], earlier_ok[None]).reshape(16, 256)

    q1 = move_ctx(q_own, lambda i: (i - 4) % 16)
    q2 = move_ctx(q_own, lambda i: (i - 8) % 16)
    q3 = move_ctx(q_own, lambda i: (i - 12) % 16)
    kv3 = move_ctx(kv2, lambda i: i ^ 1)
    kvs = (kv, kv1, kv2, kv3)
    parts = attend((1, 2, 3), flags, bias, lim, (q1, q2, q3), kvs)
    back = [move_ctx(part, lambda i: (i + 4 * dx) % 16) for dx, part in ((1, parts[0]), (2, parts[1]), (3, parts[2]))]
    (own,) = attend((0,), flags, bias, lim, (q_own,), kvs)
    sent = pl.pallas_call(
        merge_kernel,
        out_shape=jax.ShapeDtypeStruct((528, 256), BF),
        in_specs=[vmem()] * 6,
        out_specs=vmem(),
        compiler_params=grant(8),
        name="merge",
    )(own, *back, tok, gate)
    got = move_head(sent, swap)
    w_swapped = []
    for n in range(2):
        w_swapped.append(move_ctx(w_fetched[n], lambda i: i ^ 1))
    tokens = jax.ShapeDtypeStruct((512, 512), BF)
    mine = pl.pallas_call(
        place_kernel, out_shape=tokens, in_specs=[vmem()], out_specs=vmem(), compiler_params=grant(8), name="place"
    )(sent)
    theirs = pl.pallas_call(
        spread_kernel,
        out_shape=tokens,
        in_specs=[pl.BlockSpec(memory_space=pltpu.SMEM), vmem()],
        out_specs=vmem(),
        compiler_params=grant(8),
        name="spread",
    )((ctx % 2).reshape(1), got)

    def shift(step):
        return lambda i: (i // NZ) * NZ + (i % NZ + step) % NZ

    here, there = [], []
    for chunk, hops in ((0, (4, 3)), (1, (3, 4))):
        up0, up, down0, down, total = project(
            jnp.stack([y, z]), chunk, hops, mine, theirs, w_out, w_fetched[chunk], w_swapped[chunk]
        )
        total = total.astype(F32)
        for step, length, message, rest in ((1, hops[0], up0, up), (-1, hops[1], down0, down)):
            for hop in range(length):
                if hop:
                    message = (message.astype(F32) + rest[hop - 1].astype(F32)).astype(BF)
                message = move_head(message, shift(step))
            total = total + message.astype(F32)
        total = total.astype(BF)
        here.append(lax.dynamic_index_in_dim(total, y, 0, keepdims=False))
        there.append(move_head(lax.dynamic_index_in_dim(total, 1 - y, 0, keepdims=False), swap))
    low = [jnp.where(y == 0, h, t) for h, t in zip(here, there)]
    high = [jnp.where(y == 0, t, h) for h, t in zip(here, there)]
    return jnp.concatenate(low + high, axis=1)


def solution(mesh):
    placed = (
        P(("ctx", "head"), None),
        P("ctx", "head"),
        P("ctx", "head"),
        P(("ctx", "head"), None),
        P(("ctx", "head"), None),
        P(),
        P("head", None),
    )
    return jax.shard_map(layer, mesh=mesh, in_specs=placed, out_specs=P(("ctx", "head"), None), check_vma=False)
```

```python
import math

import jax
import jax.numpy as jnp
from jax import lax
from jax.experimental import pallas as pl
from jax.experimental.pallas import tpu as pltpu
from jax.sharding import PartitionSpec as P

H = 64
HD = 128
BLK = 128
CAP = 16
NX = 4
NJ = 4
NZ = 8
HALF = 2048
NEG = -1e30
SCALE2 = math.log2(math.e) / math.sqrt(HD)
BF = jnp.bfloat16
F32 = jnp.float32
NT = (((1,), (1,)), ((), ()))


def vmem():
    return pl.BlockSpec(memory_space=pltpu.VMEM)


def grant(mib):
    return pltpu.CompilerParams(vmem_limit_bytes=mib << 20)


def pack_kernel(q_ref, tgt_ref, gate_ref, out_ref):
    rows = jnp.concatenate([q_ref[:, k * HD : (k + 1) * HD] for k in range(16)], axis=0)
    tgt = tgt_ref[...]
    gate = gate_ref[...]
    hi = gate.astype(BF).astype(F32)
    mid = (gate - hi).astype(BF).astype(F32)
    tok = (lax.broadcasted_iota(jnp.int32, (1, 512), 1) % 32 + 1).astype(F32)
    aux = jnp.concatenate([tok, hi, mid, gate - hi - mid, jnp.zeros((12, 512), F32)], axis=0).astype(BF)
    for dest in range(16):
        slot = lax.broadcasted_iota(jnp.int32, (64, 512), 0) + dest * 64
        sel = jnp.where(slot == tgt, 1.0, 0.0).astype(BF)
        out_ref[dest, 0:64, :] = jnp.dot(sel, rows, preferred_element_type=F32).astype(BF)
        meta = lax.dot_general(aux, sel, NT, preferred_element_type=F32)
        meta = jnp.concatenate([meta, jnp.zeros((16, 64), F32)], axis=1)
        out_ref[dest, 64:80, :] = meta.astype(BF)


def attend_kernel(sets, flag_ref, bias_ref, lim_ref, *refs):
    count = len(sets)
    q_refs, kv_refs, out_refs = refs[:count], refs[count : count + 4], refs[count + 4 : 2 * count + 4]
    kv, sems, list_ref, done_ref, s_ref, m_ref, acc_ref = refs[2 * count + 4 :]
    copies = [pltpu.make_async_copy(src, kv.at[i], sems.at[i]) for i, src in enumerate(kv_refs)]
    for copy in copies:
        copy.start()
    copies[0].wait()
    done_ref[0] = jnp.int32(0)

    def keys_ready(last):
        for i in range(1, 4):

            @pl.when((last >= i) & (done_ref[0] < i))
            def _():
                copies[i].wait()
                done_ref[0] = jnp.int32(i)

    ones = jnp.ones((16, 256), BF)
    key_id = lax.broadcasted_iota(jnp.int32, (BLK, 256), 0).astype(F32)

    def two_blocks(q_ref, first, second, bias, lims):
        blocks = (first, second)
        state = {}

        def scores(p):
            q = q_ref[:, p * CAP : (p + 1) * CAP, :].reshape(256, HD)
            old = m_ref[p : p + 1, :]
            new = old
            for n, block in enumerate(blocks):
                k = kv[block // 4, pl.ds(pl.multiple_of((block % 4) * BLK, BLK), BLK), p * HD : (p + 1) * HD]
                s = lax.dot_general(k, q, NT, preferred_element_type=F32)
                if lims is not None:
                    s = jnp.where(key_id <= lims(p, n), s, 2.0 * NEG)
                s_ref[p, n * BLK : (n + 1) * BLK, :] = s
                top = jnp.max(s, axis=0, keepdims=True)
                new = jnp.maximum(new, top if bias is None else top + bias[n])
            m_ref[p : p + 1, :] = new
            state[p] = (new, jnp.exp2((old - new) * SCALE2))

        def values(p):
            new, factor = state[p]
            ws, vts = [], []
            for n, block in enumerate(blocks):
                base = new if bias is None else new - bias[n]
                ws.append(jnp.exp2((s_ref[p, n * BLK : (n + 1) * BLK, :] - base) * SCALE2).astype(BF))
                vts.append(kv[block // 4, 512 + p * HD : 512 + (p + 1) * HD, pl.ds(pl.multiple_of((block % 4) * BLK, BLK), BLK)])
            left = jnp.concatenate([jnp.concatenate(vts, axis=1), ones], axis=0)
            gain = jnp.dot(left, jnp.concatenate(ws, axis=0), preferred_element_type=F32)
            acc_ref[p * 144 : (p + 1) * 144, :] = acc_ref[p * 144 : (p + 1) * 144, :] * factor + gain

        scores(0)
        scores(1)
        values(0)
        scores(2)
        values(1)
        scores(3)
        values(2)
        values(3)

    for n, dx in enumerate(sets):
        q_ref, out_ref = q_refs[n], out_refs[n]
        m_ref[...] = jnp.full(m_ref.shape, NEG, F32)
        acc_ref[...] = jnp.zeros(acc_ref.shape, F32)
        if dx == 0:

            def diag_step(pair, _, q_ref=q_ref):
                def lims(p, n):
                    return lim_ref[pl.ds(p * 4 + pair * 2 + n, 1), :]

                two_blocks(q_ref, pair * 2, pair * 2 + 1, None, lims)
                return 0

            lax.fori_loop(0, 2, diag_step, 0)
        found = jnp.int32(0)
        for block in range(4 if dx == 0 else 0, 16):
            list_ref[found] = jnp.int32(block)
            found = found + flag_ref[dx, block]
        list_ref[found] = jnp.int32(16)

        def pair_step(pair, _, q_ref=q_ref, dx=dx, n=n):
            one, two = list_ref[pair * 2], list_ref[pair * 2 + 1]
            if n == 0:
                keys_ready(jnp.minimum(two, 15) // 4)
            bias = (bias_ref[pl.ds(dx * 24 + one, 1), :], bias_ref[pl.ds(dx * 24 + two, 1), :])
            two_blocks(q_ref, one, jnp.minimum(two, 15), bias, None)
            return 0

        lax.fori_loop(0, (found + 1) // 2, pair_step, 0)
        if n == 0:
            keys_ready(3)
        total = jnp.concatenate([acc_ref[p * 144 + HD : p * 144 + HD + 1, :] for p in range(4)], axis=0)
        some = total > 0.0
        safe = jnp.where(some, total, 1.0)
        inv = jnp.where(some, 1.0 / safe, 0.0)
        lse = jnp.where(some, m_ref[0:4, :] * SCALE2 + jnp.log2(safe), NEG)
        hi = lse.astype(BF)
        rest = lse - hi.astype(F32)
        mid = rest.astype(BF)
        low = (rest - mid.astype(F32)).astype(BF)
        for p in range(4):
            out_ref[p * HD : (p + 1) * HD, :] = (acc_ref[p * 144 : p * 144 + HD, :] * inv[p : p + 1, :]).astype(BF)
        out_ref[512:528, :] = jnp.concatenate([hi, mid, low, jnp.ones((4, 256), BF)], axis=0)


def attend(sets, flags, bias, lim, qs, kvs):
    part = jax.ShapeDtypeStruct((528, 256), BF)
    return pl.pallas_call(
        lambda *refs: attend_kernel(sets, *refs),
        out_shape=[part] * len(sets),
        in_specs=[pl.BlockSpec(memory_space=pltpu.SMEM)]
        + [vmem()] * (2 + len(sets))
        + [pl.BlockSpec(memory_space=pl.ANY)] * 4,
        out_specs=[vmem()] * len(sets),
        scratch_shapes=[
            pltpu.VMEM((4, 1024, 512), BF),
            pltpu.SemaphoreType.DMA((4,)),
            pltpu.SMEM((18,), jnp.int32),
            pltpu.SMEM((1,), jnp.int32),
            pltpu.VMEM((4, 256, 256), F32),
            pltpu.VMEM((8, 256), F32),
            pltpu.VMEM((576, 256), F32),
        ],
        cost_estimate=pl.CostEstimate(
            flops=len(sets) * 2 * 2 * 4 * 256 * 2048 * 128,
            bytes_accessed=5 << 20,
            transcendentals=len(sets) * 4 * 256 * 2048,
        ),
        compiler_params=grant(24),
        name="attend",
    )(flags, bias, lim, *qs, *kvs)


def place_heads(heads, pos, out_ref, lo):
    token = lax.broadcasted_iota(jnp.int32, (256, HD), 0).astype(F32)
    for r in range(2):
        place = jnp.where(token + r * 256.0 == pos[:, r * HD : (r + 1) * HD], 1.0, 0.0).astype(BF)
        out_ref[r * 256 : (r + 1) * 256, lo : lo + HD] = lax.dot_general(
            place, heads[:, r * HD : (r + 1) * HD], NT, preferred_element_type=F32
        ).astype(BF)


def slot_pos(tok):
    dev = (lax.broadcasted_iota(jnp.int32, tok.shape, 1) // CAP).astype(F32)
    return jnp.where(tok >= 0.0, dev * 32.0 + tok, -1.0)


def merge_kernel(a_ref, b_ref, c_ref, d_ref, tok_ref, gate_ref, send_ref):
    parts = (a_ref, b_ref, c_ref, d_ref)
    lses = []
    for ref in parts:
        tail = ref[512:528, :].astype(F32)
        lses.append(jnp.where(tail[12:16] > 0.5, tail[0:4] + tail[4:8] + tail[8:12], NEG))
    top = jnp.maximum(jnp.maximum(lses[0], lses[1]), jnp.maximum(lses[2], lses[3]))
    ws = [jnp.exp2(lse - top) for lse in lses]
    norm = gate_ref[...] / (ws[0] + ws[1] + ws[2] + ws[3])
    ws = [w * norm for w in ws]
    for p in range(4):
        mix = None
        for ref, w in zip(parts, ws):
            term = ref[p * HD : (p + 1) * HD, :].astype(F32) * w[p : p + 1, :]
            mix = term if mix is None else mix + term
        send_ref[p * HD : (p + 1) * HD, :] = mix.astype(BF)
    send_ref[512:528, :] = jnp.concatenate([tok_ref[...], jnp.zeros((12, 256), F32)], axis=0).astype(BF)


def place_kernel(sent_ref, out_ref):
    pos = slot_pos(sent_ref[512:528, :].astype(F32))
    for p in range(4):
        place_heads(sent_ref[p * HD : (p + 1) * HD, :], pos[p : p + 1, :], out_ref, p * HD)


def spread_kernel(core_ref, got_ref, out_ref):
    pos = slot_pos(got_ref[512:528, :].astype(F32))
    core = core_ref[0]
    for n in range(4):
        half = core if n < 2 else 1 - core
        q = n % 2
        start = pl.multiple_of(half * 256 + q * HD, HD)
        row = jnp.where(half == 0, pos[q : q + 1, :], pos[2 + q : 3 + q, :])
        place_heads(got_ref[pl.ds(start, HD), :], row, out_ref, n * HD)


def project_kernel(hops, place_ref, a_ref, b_ref, wa_ref, wb_ref, wc_ref, up0_ref, up_ref, down0_ref, down_ref, own_ref, total_ref):
    total = jnp.dot(a_ref[...], wa_ref[...], preferred_element_type=F32)
    total += jnp.dot(b_ref[:, 0:256], wb_ref[...], preferred_element_type=F32)
    total += jnp.dot(b_ref[:, 256:512], wc_ref[...], preferred_element_type=F32)
    total_ref[...] = total.astype(BF)
    z = place_ref[1]

    def rows(half, ahead):
        dest = (z + (ahead + NZ)) % NZ
        return total_ref[pl.ds(pl.multiple_of(half * 256 + dest * 32, 32), 32), :]

    for half in range(2):
        own_ref[half] = rows(half, 0)
        for step, length, first, rest in ((1, hops[0], up0_ref, up_ref), (-1, hops[1], down0_ref, down_ref)):
            first[half] = rows(half, step * length)
            for hop in range(1, length):
                rest[hop - 1, half] = rows(half, step * (length - hop))


TILE = 512
STEPS = HALF // TILE


def project(place, chunk, hops, a, b, w_out, wb, wc):
    def terms(*lead):
        return jax.ShapeDtypeStruct((*lead, 2, 32, HALF), BF)

    def block(*lead):
        zeros = (0,) * (len(lead) + 2)
        return pl.BlockSpec((*lead, 2, 32, TILE), lambda i, s: (*zeros, i))

    leads = ((), (hops[0] - 1,), (), (hops[1] - 1,), ())
    return pl.pallas_call(
        lambda *refs: project_kernel(hops, *refs),
        out_shape=[terms(*lead) for lead in leads],
        grid_spec=pltpu.PrefetchScalarGridSpec(
            num_scalar_prefetch=1,
            grid=(STEPS,),
            in_specs=[
                pl.BlockSpec((512, 512), lambda i, s: (0, 0)),
                pl.BlockSpec((512, 512), lambda i, s: (0, 0)),
                pl.BlockSpec((512, TILE), lambda i, s: (0, s[0] * (2 * STEPS) + chunk * STEPS + i)),
                pl.BlockSpec((256, TILE), lambda i, s: (0, i)),
                pl.BlockSpec((256, TILE), lambda i, s: (0, i)),
            ],
            out_specs=[block(*lead) for lead in leads],
            scratch_shapes=[pltpu.VMEM((512, TILE), BF)],
        ),
        cost_estimate=pl.CostEstimate(flops=2 * 512 * 1024 * HALF, bytes_accessed=7 << 20, transcendentals=0),
        name="project",
    )(place, a, b, w_out, wb, wc)


def layer(queries, keys, values, routes, gates, block_mask, w_out):
    ctx = lax.axis_index("ctx")
    head = lax.axis_index("head")
    x, j = ctx // NJ, ctx % NJ
    y, z = head // NZ, head % NZ

    def move_ctx(v, f):
        return lax.ppermute(v, "ctx", [(i, f(i)) for i in range(16)])

    def from_later(v, dx):
        return lax.ppermute(v, "ctx", [(i, i - NJ * dx) for i in range(NJ * dx, 16)])

    def to_later(v, dx):
        return lax.ppermute(v, "ctx", [(i, i + NJ * dx) for i in range(16 - NJ * dx)])

    def move_head(v, f):
        return lax.ppermute(v, "head", [(i, f(i)) for i in range(16)])

    def swap(i):
        return i ^ NZ

    w_fetched = []
    for n in range(2):
        given = lax.dynamic_slice(w_out, ((ctx % 2) * 256, (2 * (1 - y) + n) * HALF), (256, HALF))
        w_fetched.append(move_head(given, swap))

    kv = jnp.concatenate([keys, values.T], axis=0)
    kv2 = move_ctx(kv, lambda i: i ^ 2)
    kv1 = move_ctx(kv, lambda i: i ^ 1)

    head_ids = jnp.arange(H, dtype=jnp.int32)
    onehot = (routes[:, :, None] == head_ids[None, None, :]).astype(F32)
    per_token = jnp.sum(onehot, axis=1)
    below = (jnp.arange(32)[:, None] > jnp.arange(32)[None, :]).astype(F32)
    earlier = jnp.dot(below, per_token, preferred_element_type=F32)
    ranking = jnp.sum(onehot * earlier[:, None, :], axis=2).astype(jnp.int32)
    target = (routes * CAP + ranking).T.reshape(1, 512)
    gate_row = gates.T.reshape(1, 512)
    packed = pl.pallas_call(
        pack_kernel,
        out_shape=jax.ShapeDtypeStruct((16, 80, HD), BF),
        in_specs=[vmem()] * 3,
        out_specs=vmem(),
        compiler_params=grant(12),
        name="pack",
    )(queries, target, gate_row)
    arrived = lax.all_to_all(packed, "head", split_axis=0, concat_axis=0, tiled=True)
    q_own = arrived[:, :64, :]
    meta = arrived[:, 64:68, :64].astype(F32).reshape(16, 4, 4, CAP).transpose(1, 2, 0, 3).reshape(4, 4, 256)
    tok = meta[0] - 1.0
    gate = meta[1] + meta[2] + meta[3]
    dev = (jnp.arange(256) // CAP).astype(F32)
    in_block = jnp.maximum(tok, 0.0) + (dev[None, :] % 4.0) * 32.0

    a_id = jnp.arange(64)
    usable = (block_mask == 1) & (a_id[None, :] < a_id[:, None])
    usable = lax.dynamic_index_in_dim(usable.reshape(NX, NJ, 4, NX, NJ, 4), j, 1, keepdims=False)
    usable = lax.dynamic_index_in_dim(usable, x, 2, keepdims=False)
    usable = jnp.stack([lax.dynamic_index_in_dim(usable, j ^ i, 2, keepdims=False) for i in range(4)], axis=2)
    usable = jnp.stack([lax.dynamic_index_in_dim(usable, (x + dx) % NX, 0, keepdims=False) for dx in range(4)])
    flags = jnp.any(usable, axis=1).astype(jnp.int32).reshape(4, 16)
    bias = jnp.where(usable, 0.0, 2.0 * NEG).reshape(4, 4, 16).transpose(0, 2, 1)
    bias = jnp.concatenate([bias, jnp.full((4, 8, 4), 2.0 * NEG, F32)], axis=1)
    bias = jnp.repeat(bias, 64, axis=2).reshape(96, 256)
    same = (jnp.arange(256)[None, :] // 64) == jnp.arange(4)[:, None]
    earlier_ok = jnp.where(bias[0:4] == 0.0, 127.0, -1.0)
    lim = jnp.where(same[None], in_block[:, None, :], earlier_ok[None]).reshape(16, 256)

    q1, q2, q3 = (from_later(q_own, dx) for dx in (1, 2, 3))
    kv3 = move_ctx(kv2, lambda i: i ^ 1)
    kvs = (kv, kv1, kv2, kv3)
    back = {}
    for sets, qs in (((1, 3), (q1, q3)), ((2,), (q2,))):
        parts = attend(sets, flags, bias, lim, qs, kvs)
        for dx, part in zip(sets, parts):
            back[dx] = to_later(part, dx)
    (own,) = attend((0,), flags, bias, lim, (q_own,), kvs)
    sent = pl.pallas_call(
        merge_kernel,
        out_shape=jax.ShapeDtypeStruct((528, 256), BF),
        in_specs=[vmem()] * 6,
        out_specs=vmem(),
        compiler_params=grant(8),
        name="merge",
    )(own, back[1], back[2], back[3], tok, gate)
    got = move_head(sent, swap)
    w_swapped = []
    for n in range(2):
        w_swapped.append(move_ctx(w_fetched[n], lambda i: i ^ 1))
    tokens = jax.ShapeDtypeStruct((512, 512), BF)
    mine = pl.pallas_call(
        place_kernel, out_shape=tokens, in_specs=[vmem()], out_specs=vmem(), compiler_params=grant(8), name="place"
    )(sent)
    theirs = pl.pallas_call(
        spread_kernel,
        out_shape=tokens,
        in_specs=[pl.BlockSpec(memory_space=pltpu.SMEM), vmem()],
        out_specs=vmem(),
        compiler_params=grant(8),
        name="spread",
    )((ctx % 2).reshape(1), got)

    def shift(step):
        return lambda i: (i // NZ) * NZ + (i % NZ + step) % NZ

    here, there = [], []
    for chunk, hops in ((0, (4, 3)), (1, (3, 4))):
        up0, up, down0, down, total = project(
            jnp.stack([y, z]), chunk, hops, mine, theirs, w_out, w_fetched[chunk], w_swapped[chunk]
        )
        total = total.astype(F32)
        for step, length, message, rest in ((1, hops[0], up0, up), (-1, hops[1], down0, down)):
            for hop in range(length):
                if hop:
                    message = (message.astype(F32) + rest[hop - 1].astype(F32)).astype(BF)
                message = move_head(message, shift(step))
            total = total + message.astype(F32)
        total = total.astype(BF)
        here.append(lax.dynamic_index_in_dim(total, y, 0, keepdims=False))
        there.append(move_head(lax.dynamic_index_in_dim(total, 1 - y, 0, keepdims=False), swap))
    low = [jnp.where(y == 0, h, t) for h, t in zip(here, there)]
    high = [jnp.where(y == 0, t, h) for h, t in zip(here, there)]
    return jnp.concatenate(low + high, axis=1)


def solution(mesh):
    placed = (
        P(("ctx", "head"), None),
        P("ctx", "head"),
        P("ctx", "head"),
        P(("ctx", "head"), None),
        P(("ctx", "head"), None),
        P(),
        P("head", None),
    )
    return jax.shard_map(layer, mesh=mesh, in_specs=placed, out_specs=P(("ctx", "head"), None), check_vma=False)
```

```python
import math

import jax
import jax.numpy as jnp
from jax import lax
from jax.experimental import pallas as pl
from jax.experimental.pallas import tpu as pltpu
from jax.sharding import PartitionSpec as P

H = 64
HD = 128
BLK = 128
CAP = 16
NX = 4
NJ = 4
NZ = 8
HALF = 2048
NEG = -1e30
SCALE2 = math.log2(math.e) / math.sqrt(HD)
BF = jnp.bfloat16
F32 = jnp.float32
NT = (((1,), (1,)), ((), ()))


def vmem():
    return pl.BlockSpec(memory_space=pltpu.VMEM)


def grant(mib):
    return pltpu.CompilerParams(vmem_limit_bytes=mib << 20)


def pack_kernel(q_ref, tgt_ref, gate_ref, out_ref):
    rows = jnp.concatenate([q_ref[:, k * HD : (k + 1) * HD] for k in range(16)], axis=0)
    tgt = tgt_ref[...]
    gate = gate_ref[...]
    hi = gate.astype(BF).astype(F32)
    mid = (gate - hi).astype(BF).astype(F32)
    tok = (lax.broadcasted_iota(jnp.int32, (1, 512), 1) % 32 + 1).astype(F32)
    aux = jnp.concatenate([tok, hi, mid, gate - hi - mid, jnp.zeros((12, 512), F32)], axis=0).astype(BF)
    for dest in range(16):
        slot = lax.broadcasted_iota(jnp.int32, (64, 512), 0) + dest * 64
        sel = jnp.where(slot == tgt, 1.0, 0.0).astype(BF)
        out_ref[dest, 0:64, :] = jnp.dot(sel, rows, preferred_element_type=F32).astype(BF)
        meta = lax.dot_general(aux, sel, NT, preferred_element_type=F32)
        meta = jnp.concatenate([meta, jnp.zeros((16, 64), F32)], axis=1)
        out_ref[dest, 64:80, :] = meta.astype(BF)


def attend_kernel(sets, flag_ref, bias_ref, lim_ref, *refs):
    count = len(sets)
    q_refs, kv_refs, out_refs = refs[:count], refs[count : count + 8], refs[count + 8 : 2 * count + 8]
    kv, sems, list_ref, done_ref, s_ref, m_ref, acc_ref = refs[2 * count + 8 :]
    copies = []
    for i in range(4):
        for n in range(2):
            part = kv.at[i, n * 512 : (n + 1) * 512]
            copies.append(pltpu.make_async_copy(kv_refs[i * 2 + n], part, sems.at[i * 2 + n]))
    for copy in copies:
        copy.start()
    copies[0].wait()
    copies[1].wait()
    done_ref[0] = jnp.int32(0)

    def keys_ready(last):
        for i in range(1, 4):

            @pl.when((last >= i) & (done_ref[0] < i))
            def _():
                copies[2 * i].wait()
                copies[2 * i + 1].wait()
                done_ref[0] = jnp.int32(i)

    ones = jnp.ones((16, 256), BF)
    key_id = lax.broadcasted_iota(jnp.int32, (BLK, 256), 0).astype(F32)

    def two_blocks(q_ref, first, second, bias, lims):
        blocks = (first, second)
        state = {}

        def scores(p):
            q = q_ref[:, p * CAP : (p + 1) * CAP, :].reshape(256, HD)
            old = m_ref[p : p + 1, :]
            new = old
            for n, block in enumerate(blocks):
                k = kv[block // 4, pl.ds(pl.multiple_of((block % 4) * BLK, BLK), BLK), p * HD : (p + 1) * HD]
                s = lax.dot_general(k, q, NT, preferred_element_type=F32)
                if lims is not None:
                    s = jnp.where(key_id <= lims(p, n), s, 2.0 * NEG)
                s_ref[p, n * BLK : (n + 1) * BLK, :] = s
                top = jnp.max(s, axis=0, keepdims=True)
                new = jnp.maximum(new, top if bias is None else top + bias[n])
            m_ref[p : p + 1, :] = new
            state[p] = (new, jnp.exp2((old - new) * SCALE2))

        def values(p):
            new, factor = state[p]
            ws, vts = [], []
            for n, block in enumerate(blocks):
                base = new if bias is None else new - bias[n]
                ws.append(jnp.exp2((s_ref[p, n * BLK : (n + 1) * BLK, :] - base) * SCALE2).astype(BF))
                vts.append(kv[block // 4, 512 + p * HD : 512 + (p + 1) * HD, pl.ds(pl.multiple_of((block % 4) * BLK, BLK), BLK)])
            left = jnp.concatenate([jnp.concatenate(vts, axis=1), ones], axis=0)
            gain = jnp.dot(left, jnp.concatenate(ws, axis=0), preferred_element_type=F32)
            acc_ref[p * 144 : (p + 1) * 144, :] = acc_ref[p * 144 : (p + 1) * 144, :] * factor + gain

        scores(0)
        scores(1)
        values(0)
        scores(2)
        values(1)
        scores(3)
        values(2)
        values(3)

    for n, dx in enumerate(sets):
        q_ref, out_ref = q_refs[n], out_refs[n]
        m_ref[...] = jnp.full(m_ref.shape, NEG, F32)
        acc_ref[...] = jnp.zeros(acc_ref.shape, F32)
        if dx == 0:

            def diag_step(pair, _, q_ref=q_ref):
                def lims(p, n):
                    return lim_ref[pl.ds(p * 4 + pair * 2 + n, 1), :]

                two_blocks(q_ref, pair * 2, pair * 2 + 1, None, lims)
                return 0

            lax.fori_loop(0, 2, diag_step, 0)
        found = jnp.int32(0)
        for block in range(4 if dx == 0 else 0, 16):
            list_ref[found] = jnp.int32(block)
            found = found + flag_ref[dx, block]
        list_ref[found] = jnp.int32(16)

        def pair_step(pair, _, q_ref=q_ref, dx=dx, n=n):
            one, two = list_ref[pair * 2], list_ref[pair * 2 + 1]
            if n == 0:
                keys_ready(jnp.minimum(two, 15) // 4)
            bias = (bias_ref[pl.ds(dx * 24 + one, 1), :], bias_ref[pl.ds(dx * 24 + two, 1), :])
            two_blocks(q_ref, one, jnp.minimum(two, 15), bias, None)
            return 0

        lax.fori_loop(0, (found + 1) // 2, pair_step, 0)
        if n == 0:
            keys_ready(3)
        total = jnp.concatenate([acc_ref[p * 144 + HD : p * 144 + HD + 1, :] for p in range(4)], axis=0)
        some = total > 0.0
        safe = jnp.where(some, total, 1.0)
        inv = jnp.where(some, 1.0 / safe, 0.0)
        lse = jnp.where(some, m_ref[0:4, :] * SCALE2 + jnp.log2(safe), NEG)
        hi = lse.astype(BF)
        rest = lse - hi.astype(F32)
        mid = rest.astype(BF)
        low = (rest - mid.astype(F32)).astype(BF)
        for p in range(4):
            out_ref[p * HD : (p + 1) * HD, :] = (acc_ref[p * 144 : p * 144 + HD, :] * inv[p : p + 1, :]).astype(BF)
        out_ref[512:528, :] = jnp.concatenate([hi, mid, low, jnp.ones((4, 256), BF)], axis=0)


def attend(sets, flags, bias, lim, qs, kvs):
    part = jax.ShapeDtypeStruct((528, 256), BF)
    return pl.pallas_call(
        lambda *refs: attend_kernel(sets, *refs),
        out_shape=[part] * len(sets),
        in_specs=[pl.BlockSpec(memory_space=pltpu.SMEM)]
        + [vmem()] * (2 + len(sets))
        + [pl.BlockSpec(memory_space=pl.ANY)] * 8,
        out_specs=[vmem()] * len(sets),
        scratch_shapes=[
            pltpu.VMEM((4, 1024, 512), BF),
            pltpu.SemaphoreType.DMA((8,)),
            pltpu.SMEM((18,), jnp.int32),
            pltpu.SMEM((1,), jnp.int32),
            pltpu.VMEM((4, 256, 256), F32),
            pltpu.VMEM((8, 256), F32),
            pltpu.VMEM((576, 256), F32),
        ],
        cost_estimate=pl.CostEstimate(
            flops=len(sets) * 2 * 2 * 4 * 256 * 2048 * 128,
            bytes_accessed=5 << 20,
            transcendentals=len(sets) * 4 * 256 * 2048,
        ),
        compiler_params=grant(24),
        name="attend",
    )(flags, bias, lim, *qs, *kvs)


def place_heads(heads, pos, out_ref, lo):
    token = lax.broadcasted_iota(jnp.int32, (256, HD), 0).astype(F32)
    for r in range(2):
        place = jnp.where(token + r * 256.0 == pos[:, r * HD : (r + 1) * HD], 1.0, 0.0).astype(BF)
        out_ref[r * 256 : (r + 1) * 256, lo : lo + HD] = lax.dot_general(
            place, heads[:, r * HD : (r + 1) * HD], NT, preferred_element_type=F32
        ).astype(BF)


def slot_pos(tok):
    dev = (lax.broadcasted_iota(jnp.int32, tok.shape, 1) // CAP).astype(F32)
    return jnp.where(tok >= 0.0, dev * 32.0 + tok, -1.0)


def merge_kernel(a_ref, b_ref, c_ref, d_ref, tok_ref, gate_ref, send_ref):
    parts = (a_ref, b_ref, c_ref, d_ref)
    lses = []
    for ref in parts:
        tail = ref[512:528, :].astype(F32)
        lses.append(jnp.where(tail[12:16] > 0.5, tail[0:4] + tail[4:8] + tail[8:12], NEG))
    top = jnp.maximum(jnp.maximum(lses[0], lses[1]), jnp.maximum(lses[2], lses[3]))
    ws = [jnp.exp2(lse - top) for lse in lses]
    norm = gate_ref[...] / (ws[0] + ws[1] + ws[2] + ws[3])
    ws = [w * norm for w in ws]
    for p in range(4):
        mix = None
        for ref, w in zip(parts, ws):
            term = ref[p * HD : (p + 1) * HD, :].astype(F32) * w[p : p + 1, :]
            mix = term if mix is None else mix + term
        send_ref[p * HD : (p + 1) * HD, :] = mix.astype(BF)
    send_ref[512:528, :] = jnp.concatenate([tok_ref[...], jnp.zeros((12, 256), F32)], axis=0).astype(BF)


def place_kernel(at_ref, sent_ref, out_ref):
    pos = slot_pos(sent_ref[512:528, :].astype(F32))
    for p in range(4):
        place_heads(sent_ref[p * HD : (p + 1) * HD, :], pos[p : p + 1, :], out_ref, p * HD)


def spread_kernel(at_ref, got_ref, out_ref):
    pos = slot_pos(got_ref[512:528, :].astype(F32))
    core = at_ref[2]
    for n in range(4):
        half = core if n < 2 else 1 - core
        q = n % 2
        start = pl.multiple_of(half * 256 + q * HD, HD)
        row = jnp.where(half == 0, pos[q : q + 1, :], pos[2 + q : 3 + q, :])
        place_heads(got_ref[pl.ds(start, HD), :], row, out_ref, n * HD)


def project_kernel(hops, place_ref, a_ref, b_ref, wa_ref, wb_ref, wc_ref, up0_ref, up_ref, down0_ref, down_ref, own_ref, total_ref):
    total = jnp.dot(a_ref[...], wa_ref[...], preferred_element_type=F32)
    total += jnp.dot(b_ref[:, 0:256], wb_ref[...], preferred_element_type=F32)
    total += jnp.dot(b_ref[:, 256:512], wc_ref[...], preferred_element_type=F32)
    total_ref[...] = total.astype(BF)
    z = place_ref[1]

    def rows(half, ahead):
        dest = (z + (ahead + NZ)) % NZ
        return total_ref[pl.ds(pl.multiple_of(half * 256 + dest * 32, 32), 32), :]

    for half in range(2):
        own_ref[half] = rows(half, 0)
        for step, length, first, rest in ((1, hops[0], up0_ref, up_ref), (-1, hops[1], down0_ref, down_ref)):
            first[half] = rows(half, step * length)
            for hop in range(1, length):
                rest[hop - 1, half] = rows(half, step * (length - hop))


TILE = 512
STEPS = HALF // TILE


def project(place, chunk, hops, a, b, w_out, wb, wc):
    def terms(*lead):
        return jax.ShapeDtypeStruct((*lead, 2, 32, HALF), BF)

    def block(*lead):
        zeros = (0,) * (len(lead) + 2)
        return pl.BlockSpec((*lead, 2, 32, TILE), lambda i, s: (*zeros, i))

    leads = ((), (hops[0] - 1,), (), (hops[1] - 1,), ())
    return pl.pallas_call(
        lambda *refs: project_kernel(hops, *refs),
        out_shape=[terms(*lead) for lead in leads],
        grid_spec=pltpu.PrefetchScalarGridSpec(
            num_scalar_prefetch=1,
            grid=(STEPS,),
            in_specs=[
                pl.BlockSpec((512, 512), lambda i, s: (0, 0)),
                pl.BlockSpec((512, 512), lambda i, s: (0, 0)),
                pl.BlockSpec((512, TILE), lambda i, s: (0, s[0] * (2 * STEPS) + chunk * STEPS + i)),
                pl.BlockSpec((256, TILE), lambda i, s: (0, i)),
                pl.BlockSpec((256, TILE), lambda i, s: (0, i)),
            ],
            out_specs=[block(*lead) for lead in leads],
            scratch_shapes=[pltpu.VMEM((512, TILE), BF)],
        ),
        compiler_params=grant(56),
        cost_estimate=pl.CostEstimate(flops=2 * 512 * 1024 * HALF, bytes_accessed=7 << 20, transcendentals=0),
        name="project",
    )(place, a, b, w_out, wb, wc)


def layer(queries, keys, values, routes, gates, block_mask, w_out):
    ctx = lax.axis_index("ctx")
    head = lax.axis_index("head")
    x, j = ctx // NJ, ctx % NJ
    y, z = head // NZ, head % NZ

    def move_ctx(v, f):
        return lax.ppermute(v, "ctx", [(i, f(i)) for i in range(16)])

    def from_later(v, dx):
        return lax.ppermute(v, "ctx", [(i, i - NJ * dx) for i in range(NJ * dx, 16)])

    def to_later(v, dx):
        return lax.ppermute(v, "ctx", [(i, i + NJ * dx) for i in range(16 - NJ * dx)])

    def move_head(v, f):
        return lax.ppermute(v, "head", [(i, f(i)) for i in range(16)])

    def swap(i):
        return i ^ NZ

    w_fetched = []
    for n in range(2):
        given = lax.dynamic_slice(w_out, ((ctx % 2) * 256, (2 * (1 - y) + n) * HALF), (256, HALF))
        w_fetched.append(move_head(given, swap))

    def partners(v):
        return move_ctx(v, lambda i: i ^ 2), move_ctx(v, lambda i: i ^ 1)

    turned = values.T
    k2, k1 = partners(keys)
    v2, v1 = partners(turned)

    head_ids = jnp.arange(H, dtype=jnp.int32)
    onehot = (routes[:, :, None] == head_ids[None, None, :]).astype(F32)
    per_token = jnp.sum(onehot, axis=1)
    below = (jnp.arange(32)[:, None] > jnp.arange(32)[None, :]).astype(F32)
    earlier = jnp.dot(below, per_token, preferred_element_type=F32)
    ranking = jnp.sum(onehot * earlier[:, None, :], axis=2).astype(jnp.int32)
    target = (routes * CAP + ranking).T.reshape(1, 512)
    gate_row = gates.T.reshape(1, 512)
    packed = pl.pallas_call(
        pack_kernel,
        out_shape=jax.ShapeDtypeStruct((16, 80, HD), BF),
        in_specs=[vmem()] * 3,
        out_specs=vmem(),
        name="pack",
    )(queries, target, gate_row)
    arrived = lax.all_to_all(packed, "head", split_axis=0, concat_axis=0, tiled=True)
    q_own = arrived[:, :64, :]
    meta = arrived[:, 64:68, :64].astype(F32).reshape(16, 4, 4, CAP).transpose(1, 2, 0, 3).reshape(4, 4, 256)
    tok = meta[0] - 1.0
    gate = meta[1] + meta[2] + meta[3]
    dev = (jnp.arange(256) // CAP).astype(F32)
    in_block = jnp.maximum(tok, 0.0) + (dev[None, :] % 4.0) * 32.0

    a_id = jnp.arange(64)
    usable = (block_mask == 1) & (a_id[None, :] < a_id[:, None])
    usable = lax.dynamic_index_in_dim(usable.reshape(NX, NJ, 4, NX, NJ, 4), j, 1, keepdims=False)
    usable = lax.dynamic_index_in_dim(usable, x, 2, keepdims=False)
    usable = jnp.stack([lax.dynamic_index_in_dim(usable, j ^ i, 2, keepdims=False) for i in range(4)], axis=2)
    usable = jnp.stack([lax.dynamic_index_in_dim(usable, (x + dx) % NX, 0, keepdims=False) for dx in range(4)])
    flags = jnp.any(usable, axis=1).astype(jnp.int32).reshape(4, 16)
    bias = jnp.where(usable, 0.0, 2.0 * NEG).reshape(4, 4, 16).transpose(0, 2, 1)
    bias = jnp.concatenate([bias, jnp.full((4, 8, 4), 2.0 * NEG, F32)], axis=1)
    bias = jnp.repeat(bias, 64, axis=2).reshape(96, 256)
    same = (jnp.arange(256)[None, :] // 64) == jnp.arange(4)[:, None]
    earlier_ok = jnp.where(bias[0:4] == 0.0, 127.0, -1.0)
    lim = jnp.where(same[None], in_block[:, None, :], earlier_ok[None]).reshape(16, 256)

    q1, q2, q3 = (from_later(q_own, dx) for dx in (1, 2, 3))
    k3, v3 = move_ctx(k2, lambda i: i ^ 1), move_ctx(v2, lambda i: i ^ 1)
    kvs = (keys, turned, k1, v1, k2, v2, k3, v3)
    back = {}
    for sets, qs in (((1, 3), (q1, q3)), ((2,), (q2,))):
        parts = attend(sets, flags, bias, lim, qs, kvs)
        for dx, part in zip(sets, parts):
            back[dx] = to_later(part, dx)
    (own,) = attend((0,), flags, bias, lim, (q_own,), kvs)
    sent = pl.pallas_call(
        merge_kernel,
        out_shape=jax.ShapeDtypeStruct((528, 256), BF),
        in_specs=[vmem()] * 6,
        out_specs=vmem(),
        compiler_params=grant(8),
        name="merge",
    )(own, back[1], back[2], back[3], tok, gate)
    got = move_head(sent, swap)
    w_swapped = []
    for n in range(2):
        w_swapped.append(move_ctx(w_fetched[n], lambda i: i ^ 1))
    tokens = jax.ShapeDtypeStruct((512, 512), BF)
    at = jnp.stack([y, z, ctx % 2])
    mine = pl.pallas_call(
        place_kernel, out_shape=tokens, in_specs=[pl.BlockSpec(memory_space=pltpu.SMEM), vmem()], out_specs=vmem(), compiler_params=grant(8), name="place"
    )(at, sent)
    theirs = pl.pallas_call(
        spread_kernel,
        out_shape=tokens,
        in_specs=[pl.BlockSpec(memory_space=pltpu.SMEM), vmem()],
        out_specs=vmem(),
        compiler_params=grant(8),
        name="spread",
    )(at, got)

    def shift(step):
        return lambda i: (i // NZ) * NZ + (i % NZ + step) % NZ

    here, there = [], []
    for chunk, hops in ((0, (4, 3)), (1, (3, 4))):
        up0, up, down0, down, total = project(at, chunk, hops, mine, theirs, w_out, w_fetched[chunk], w_swapped[chunk])
        total = total.astype(F32)
        for step, length, message, rest in ((1, hops[0], up0, up), (-1, hops[1], down0, down)):
            for hop in range(length):
                if hop:
                    message = (message.astype(F32) + rest[hop - 1].astype(F32)).astype(BF)
                message = move_head(message, shift(step))
            total = total + message.astype(F32)
        total = total.astype(BF)
        here.append(lax.dynamic_index_in_dim(total, y, 0, keepdims=False))
        there.append(move_head(lax.dynamic_index_in_dim(total, 1 - y, 0, keepdims=False), swap))
    low = [jnp.where(y == 0, h, t) for h, t in zip(here, there)]
    high = [jnp.where(y == 0, t, h) for h, t in zip(here, there)]
    return jnp.concatenate(low + high, axis=1)


def solution(mesh):
    placed = (
        P(("ctx", "head"), None),
        P("ctx", "head"),
        P("ctx", "head"),
        P(("ctx", "head"), None),
        P(("ctx", "head"), None),
        P(),
        P("head", None),
    )
    return jax.shard_map(layer, mesh=mesh, in_specs=placed, out_specs=P(("ctx", "head"), None), check_vma=False)
```
